32 devices in a mesh: section: 4 (over x, core), col: 4 (over z), row: 2 (over y).
Axes of the slice: x: 2, y: 2, z: 4, core: 2. Of those that a mesh axis runs over, the one named last changes fastest.
Arguments:
- features: bfloat16 [4, 32, 128, 256], P(None, 'row', 'col'), may hold values from -6 to 6
- conv_weight: bfloat16 [4, 3, 3, 256, 256], P('section'), may hold values from -0.125 to 0.125
- tissue: int32 [4, 32, 128], P(None, 'row', 'col'), may hold values 0 or 1
Outputs:
- section_out: bfloat16 [4, 4, 32, 128, 256], P('section', None, 'row', 'col')
- loss_map: float32 [4, 4, 32, 128], P('section', None, 'row', 'col')
The draws below stay inside these ranges and needn't reach their ends.
All inputs are finite; a program needn't handle non-finite values. No bound on the sum of `tissue` on one device may be relied on, other than what follows from the above.
Results may differ from the reference program's by a relative error of at most 0.008.
Values may be sent and summed in bfloat16 or wider, within the bound.
A program may use at most 64 MiB of HBM per device.

```python
import jax
import jax.numpy as jnp
from jax import lax

C = 256
DILATION_RATE = 2
MICRO = 4
LAYERS = 4
H = 32
W = 128


def place_ends(values, rng, least, high):
    extent = values.shape
    place = [jax.random.randint(jax.random.fold_in(rng, axis), (), 0, extent[axis]) for axis in range(len(extent))]
    values = values.at[tuple(place)].set(least)
    longest = extent.index(max(extent))
    place[longest] = (place[longest] + 1) % extent[longest]
    return values.at[tuple(place)].set(high)


def levels(stream_key, dims, cuts, smallest, top_value):
    factor_of = 1.0
    for position, shards_of in cuts:
        heights = jax.random.uniform(jax.random.fold_in(jax.random.fold_in(stream_key, 6), position), (shards_of,), jnp.float32, smallest / len(cuts), top_value / len(cuts))
        factor_of = factor_of * jnp.repeat(jnp.exp(heights), dims[position] // shards_of).reshape((-1,) + (1,) * (len(dims) - 1 - position))
    return factor_of


def bell_draw(own_key, dims, spread, reach, pieces=(), dtype=jnp.bfloat16):
    values = jax.random.normal(own_key, dims, jnp.float32) * spread
    if len(pieces) > 0:
        values = levels(own_key, dims, pieces, -0.22, 0.18) * values
    return jnp.clip(values, min=-reach, max=reach).astype(dtype)


def setup_inputs(seed: int = 0) -> dict:
    arg_keys = jax.random.split(jax.random.key(seed), 4)
    features = bell_draw(arg_keys[0], (MICRO, H, W, C), 1.0, 6.0, ((1, 2), (2, 4)))
    conv_weight = bell_draw(arg_keys[1], (LAYERS, 3, 3, C, C), (9 * C) ** -0.5, 0.125, ((0, 4),))
    tissue = place_ends((jax.random.randint(arg_keys[2], (MICRO, H, W), 0, 2) < 1).astype(jnp.int32), jax.random.fold_in(arg_keys[2], 1), 0, 1)
    return {"features": features, "conv_weight": conv_weight, "tissue": tissue}


residual_scale = 0.8


def apply_layer(current_activation, filter_weight):
    hidden_features = lax.conv_general_dilated(current_activation.astype(jnp.float32), filter_weight.astype(jnp.float32), (1, 1), ((DILATION_RATE, DILATION_RATE), (DILATION_RATE, DILATION_RATE)), rhs_dilation=(DILATION_RATE, DILATION_RATE), dimension_numbers=("NHWC", "HWIO", "NHWC"), precision=lax.Precision.HIGHEST)
    return (residual_scale * (current_activation.astype(jnp.float32) + jnp.maximum(hidden_features, 0.0))).astype(jnp.bfloat16)


def reference(features, conv_weight, tissue):
    flipped = features[:, :, ::-1, :]
    current_activation = jnp.stack([features, flipped], 1).reshape(MICRO * 2, H, W, C)
    stacked_out = []
    losses = []
    mask_float = tissue.astype(jnp.float32)
    for layer_index in range(LAYERS):
        current_activation = apply_layer(current_activation, conv_weight[layer_index])
        split_pairs = current_activation.reshape(MICRO, 2, H, W, C)
        primary = split_pairs[:, 0]
        restored = split_pairs[:, 1][:, :, ::-1, :]
        deviation = primary.astype(jnp.float32) - restored.astype(jnp.float32)
        losses.append(mask_float * jnp.mean(deviation * deviation, -1))
        stacked_out.append(primary)
    return jnp.stack(stacked_out), jnp.stack(losses)
```

```python
import functools

import jax
import jax.numpy as jnp
from jax import lax
from jax.experimental import pallas as pl
from jax.experimental.pallas import tpu as pltpu
from jax.sharding import PartitionSpec as P

DILATION_RATE = 2
TAPS = 3
PIECES = 3
residual_scale = 0.8
MESH = pl.DeviceIdType.MESH


def kernel(cfg, f_ref, w_ref, out_ref, loss_ref, fwin, wall, act, stage, lstage,
           hs_sem, hr_sem, xs_sem, xr_sem, ys_sem, yr_sem, bs_sem, br_sem, cs_sem, cr_sem,
           os_sem, or_sem, ls_sem, lr_sem, loc_sem):
    S, M, R, CL, C, n_col, halo, hb, NR, NC = cfg
    me = lax.axis_index("section")
    col = lax.axis_index("col")
    row = lax.axis_index("row")
    micro = lax.rem(me, M)
    group = S // M
    replica = me // M
    sib = me + 1 - 2 * lax.rem(me, 2)
    pairs = S // 2
    my_pair = me // 2
    low = lax.rem(me, 2)
    other_row = 1 - row
    has_left = col > 0
    has_right = col < n_col - 1

    def at(section=None, c=None, r=None):
        return {
            "section": me if section is None else section,
            "col": col if c is None else c,
            "row": row if r is None else r,
        }

    barrier = pltpu.get_barrier_semaphore()

    def hello(dev):
        pl.semaphore_signal(barrier, inc=1, device_id=dev, device_id_type=MESH)

    for d in range(1, S):
        hello(at(section=lax.rem(me + d, S)))
    hello(at(r=other_row))

    @pl.when(has_left)
    def _():
        hello(at(c=col - 1))
        hello(at(c=col - 1, r=other_row))

    @pl.when(has_right)
    def _():
        hello(at(c=col + 1))
        hello(at(c=col + 1, r=other_row))

    K = w_ref.shape[0]
    half = K // 2
    piece = half // PIECES

    own_w = pltpu.make_async_copy(w_ref, wall.at[me], loc_sem.at[0])
    own_w.start()
    own_f = pltpu.make_async_copy(
        f_ref.at[micro],
        fwin.at[pl.ds(row * halo, R), pl.ds(hb, CL)],
        loc_sem.at[1],
    )
    own_f.start()

    for b in range(2):
        for mem in range(2):
            zeros = jnp.zeros((DILATION_RATE * NC, TAPS * C), jnp.bfloat16)
            act[b, mem, 0 : DILATION_RATE * NC, :] = zeros
            act[b, mem, (DILATION_RATE + NR) * NC :, :] = zeros

    greeted = 1 + (S - 1) + 2 * has_left.astype(jnp.int32) + 2 * has_right.astype(jnp.int32)
    pl.semaphore_wait(barrier, greeted)

    def remote(src, dst, s_sem, r_sem, dev):
        return pltpu.make_async_remote_copy(
            src_ref=src, dst_ref=dst, send_sem=s_sem, recv_sem=r_sem,
            device_id=dev, device_id_type=MESH,
        )

    rows_here = pl.ds(row * halo, R)
    rows_out = pl.ds((1 - row) * (R - halo), halo)
    rows_in = pl.ds(row * R, halo)
    mid = pl.ds(hb, CL)
    lcols, rcols = pl.ds(0, hb), pl.ds(hb + CL, hb)
    first, last = pl.ds(0, hb), pl.ds(CL - hb, hb)
    mine = f_ref.at[micro]
    to_left = remote(mine.at[:, first], fwin.at[rows_here, rcols], hs_sem.at[0], hr_sem.at[0], at(c=col - 1))
    to_right = remote(mine.at[:, last], fwin.at[rows_here, lcols], hs_sem.at[1], hr_sem.at[1], at(c=col + 1))
    to_row = remote(mine.at[rows_out], fwin.at[rows_in, mid], hs_sem.at[2], hr_sem.at[2], at(r=other_row))
    to_dl = remote(mine.at[rows_out, first], fwin.at[rows_in, rcols], hs_sem.at[3], hr_sem.at[3], at(c=col - 1, r=other_row))
    to_dr = remote(mine.at[rows_out, last], fwin.at[rows_in, lcols], hs_sem.at[4], hr_sem.at[4], at(c=col + 1, r=other_row))
    to_row.start()

    @pl.when(has_left)
    def _():
        to_left.start()
        to_dl.start()

    @pl.when(has_right)
    def _():
        to_right.start()
        to_dr.start()

    to_sib = remote(w_ref, wall.at[me], bs_sem, br_sem, at(section=sib))
    to_sib.start()

    def twin(k):
        a, b, res, bit = my_pair, k, 0, 1
        while bit < pairs:
            res = res + bit * lax.rem(a // bit + b // bit, 2)
            bit *= 2
        return 2 * res + low

    def part(h, j):
        return pl.ds(pl.multiple_of(h * half + j * piece, 16), piece)

    xcopies = {}
    for k in range(1, pairs):
        for j in range(PIECES):
            cp = remote(w_ref.at[part(row, j)], wall.at[me, part(row, j)],
                        xs_sem.at[k, j], xr_sem.at[k, j], at(section=twin(k)))
            cp.start()
            xcopies[k, j] = cp

    def gather(k):
        t = twin(k)
        tsib = t + 1 - 2 * low
        ycopies, ccopies = [], []
        for j in range(PIECES):
            slot = wall.at[t, part(row, j)]
            remote(slot, slot, xs_sem.at[k, j], xr_sem.at[k, j], at(section=t)).wait_recv()
            cp = remote(slot, slot, ys_sem.at[k, j], yr_sem.at[k, j], at(r=other_row))
            cp.start()
            ycopies.append(cp)
            cp = remote(slot, slot, cs_sem.at[k, 0, j], cr_sem.at[k, 0, j], at(section=sib))
            cp.start()
            ccopies.append(cp)
        for j in range(PIECES):
            slot = wall.at[t, part(other_row, j)]
            remote(slot, slot, ys_sem.at[k, j], yr_sem.at[k, j], at(r=other_row)).wait_recv()
            cp = remote(slot, slot, cs_sem.at[k, 1, j], cr_sem.at[k, 1, j], at(section=sib))
            cp.start()
            ccopies.append(cp)
        for h in range(2):
            for j in range(PIECES):
                slot = wall.at[tsib, part(row if h == 0 else other_row, j)]
                remote(slot, slot, cs_sem.at[k, h, j], cr_sem.at[k, h, j], at(section=sib)).wait_recv()
        for cp in ycopies + ccopies:
            cp.wait_send()

    own_f.wait()
    to_row.wait()

    @pl.when(has_left)
    def _():
        to_left.wait_send()
        to_dl.wait_send()
        to_right.wait_recv()
        to_dr.wait_recv()

    @pl.when(has_right)
    def _():
        to_right.wait_send()
        to_dr.wait_send()
        to_left.wait_recv()
        to_dl.wait_recv()

    cpos = lax.broadcasted_iota(jnp.int32, (1, NC, C), 1) + (col * CL - halo)
    in_map = jnp.logical_and(cpos >= 0, cpos < n_col * CL)

    def put(b, mem, at_row, y, rows):
        m = rows * NC
        sl = pl.ds(pl.multiple_of((at_row + DILATION_RATE) * NC, 16), m)
        left = pltpu.roll(y, DILATION_RATE, 0).astype(jnp.bfloat16)
        right = pltpu.roll(y, m - DILATION_RATE, 0).astype(jnp.bfloat16)
        center = y.astype(jnp.bfloat16)
        for mm in mem:
            act[b, mm, sl, 0:C] = left if mm == 0 else right
            act[b, mm, sl, C : 2 * C] = center
            act[b, mm, sl, 2 * C : 3 * C] = right if mm == 0 else left

    off = hb - halo
    for i in range(0, NR, 4):
        v = fwin[i : i + 4].astype(jnp.float32)[:, off : off + NC, :]
        v = jnp.where(in_map, v, 0.0)
        put(0, (0, 1), i, v.reshape(4 * NC, C), 4)

    own_w.wait()
    to_sib.wait()

    for l in range(S):
        if l % 2 == 0:
            for k in range(1, pairs):
                @pl.when(twin(k) // 2 == l // 2)
                def _(k=k):
                    gather(k)
        n = NR - DILATION_RATE * (l + 1)
        r0 = row * (NR - n)
        chunk = n // 2
        m = chunk * NC
        cur, nxt = l % 2, (l + 1) % 2
        for q in range(2):
            base = r0 + q * chunk
            ys = []
            for mem in range(2):
                lhs = jnp.concatenate(
                    [act[cur, mem, pl.ds(pl.multiple_of((base + DILATION_RATE * ky) * NC, 16), m), :] for ky in range(TAPS)],
                    axis=1,
                )
                acc = jnp.dot(lhs, wall[l], preferred_element_type=jnp.float32)
                res = act[cur, mem, pl.ds(pl.multiple_of((base + DILATION_RATE) * NC, 16), m), C : 2 * C]
                y = residual_scale * (res.astype(jnp.float32) + jnp.maximum(acc, 0.0))
                y = jnp.where(in_map, y.reshape(chunk, NC, C), 0.0)
                y = y.astype(jnp.bfloat16).astype(jnp.float32)
                if l < S - 1:
                    put(nxt, (mem,), base, y.reshape(m, C), chunk)
                ys.append(y[:, halo : halo + CL, :])
            stage[l, q * chunk : (q + 1) * chunk] = ys[0].astype(jnp.bfloat16)
            d = ys[0] - ys[1]
            lstage[l, q * chunk : (q + 1) * chunk, 0:CL] = jnp.sum(d * d, axis=-1)

        src = stage.at[l, pl.ds(row * (n - R), R)]

        @pl.when(jnp.logical_and(replica == l % group, me != l))
        def _(l=l, src=src):
            remote(src, out_ref.at[micro], os_sem.at[l], or_sem.at[micro], at(section=l)).start()
            remote(lstage.at[l], loss_ref.at[micro], ls_sem.at[l], lr_sem.at[micro], at(section=l)).start()

        @pl.when(jnp.logical_and(replica == l % group, me == l))
        def _(l=l, src=src):
            pltpu.make_async_copy(src, out_ref.at[micro], loc_sem.at[2]).start()
            pltpu.make_async_copy(lstage.at[l], loss_ref.at[micro], loc_sem.at[3]).start()

    for k in range(1, pairs):
        for j in range(PIECES):
            xcopies[k, j].wait_send()

    for l in range(S):
        n = NR - DILATION_RATE * (l + 1)
        src = stage.at[l, pl.ds(row * (n - R), R)]

        @pl.when(jnp.logical_and(replica == l % group, me != l))
        def _(l=l, src=src):
            remote(src, out_ref.at[micro], os_sem.at[l], or_sem.at[micro], at(section=l)).wait_send()
            remote(lstage.at[l], loss_ref.at[micro], ls_sem.at[l], lr_sem.at[micro], at(section=l)).wait_send()

        @pl.when(jnp.logical_and(replica == l % group, me == l))
        def _(l=l, src=src):
            pltpu.make_async_copy(src, out_ref.at[micro], loc_sem.at[2]).wait()
            pltpu.make_async_copy(lstage.at[l], loss_ref.at[micro], loc_sem.at[3]).wait()

    for b in range(M):
        sender = b + M * lax.rem(me, group)

        @pl.when(sender != me)
        def _(b=b, sender=sender):
            remote(out_ref.at[b], out_ref.at[b], os_sem.at[0], or_sem.at[b], at(section=sender)).wait_recv()
            remote(loss_ref.at[b], loss_ref.at[b], ls_sem.at[0], lr_sem.at[b], at(section=sender)).wait_recv()


def local(features, conv_weight, tissue):
    S = lax.axis_size("section")
    n_col = lax.axis_size("col")
    M, R, CL, C = features.shape
    halo = DILATION_RATE * S
    hb = -(-halo // 16) * 16
    NR, NC = R + halo, CL + 2 * halo
    taps = conv_weight.shape[1]
    K = taps * taps * C
    pairs = S // 2
    lanes = -(-CL // 128) * 128
    cfg = (S, M, R, CL, C, n_col, halo, hb, NR, NC)
    anyspec = pl.BlockSpec(memory_space=pl.ANY)
    dma = pltpu.SemaphoreType.DMA
    out, sums = pl.pallas_call(
        functools.partial(kernel, cfg),
        out_shape=(
            jax.ShapeDtypeStruct((M, R, CL, C), jnp.bfloat16),
            jax.ShapeDtypeStruct((M, NR, lanes), jnp.float32),
        ),
        in_specs=[anyspec, anyspec],
        out_specs=(anyspec, anyspec),
        scratch_shapes=[
            pltpu.VMEM((NR, CL + 2 * hb, C), jnp.bfloat16),
            pltpu.VMEM((S, K, C), jnp.bfloat16),
            pltpu.VMEM((2, 2, (NR + 2 * DILATION_RATE) * NC, taps * C), jnp.bfloat16),
            pltpu.VMEM((S, NR, CL, C), jnp.bfloat16),
            pltpu.VMEM((S, NR, lanes), jnp.float32),
            dma((5,)), dma((5,)),
            dma((pairs, PIECES)), dma((pairs, PIECES)),
            dma((pairs, PIECES)), dma((pairs, PIECES)),
            dma, dma,
            dma((pairs, 2, PIECES)), dma((pairs, 2, PIECES)),
            dma((S,)), dma((M,)),
            dma((S,)), dma((M,)),
            dma((4,)),
        ],
        compiler_params=pltpu.CompilerParams(
            collective_id=0, has_side_effects=True, vmem_limit_bytes=60 * 1024 * 1024
        ),
    )(features, conv_weight.reshape(K, C))
    layer = lax.axis_index("section")
    start = lax.axis_index("row") * (halo - DILATION_RATE * (layer + 1))
    own = lax.dynamic_slice_in_dim(sums, start, R, axis=1)[:, :, :CL]
    loss = tissue.astype(jnp.float32) * (own * (1.0 / C))
    return out[None], loss[None]


def solution(mesh):
    return jax.shard_map(
        local,
        mesh=mesh,
        in_specs=(
            P(None, "row", "col", None),
            P("section", None, None, None, None),
            P(None, "row", "col"),
        ),
        out_specs=(P("section", None, "row", "col", None), P("section", None, "row", "col")),
        check_vma=False,
    )
```

```python
import functools

import jax
import jax.numpy as jnp
from jax import lax
from jax.experimental import pallas as pl
from jax.experimental.pallas import tpu as pltpu
from jax.sharding import PartitionSpec as P

DILATION_RATE = 2
TAPS = 3
PIECES = 6
residual_scale = 0.8
MESH = pl.DeviceIdType.MESH


def kernel(cfg, f_ref, w_ref, out_ref, loss_ref, fwin, wall, act, stage, lstage,
           hs_sem, hr_sem, xs_sem, xr_sem, ys_sem, yr_sem, bs_sem, br_sem, cs_sem, cr_sem,
           os_sem, or_sem, ls_sem, lr_sem, loc_sem):
    S, M, R, CL, C, n_col, halo, hb, NR, NC = cfg
    me = lax.axis_index("section")
    col = lax.axis_index("col")
    row = lax.axis_index("row")
    micro = lax.rem(me, M)
    group = S // M
    replica = me // M
    sib = me + 1 - 2 * lax.rem(me, 2)
    pairs = S // 2
    my_pair = me // 2
    low = lax.rem(me, 2)
    other_row = 1 - row
    has_left = col > 0
    has_right = col < n_col - 1

    def at(section=None, c=None, r=None):
        return {
            "section": me if section is None else section,
            "col": col if c is None else c,
            "row": row if r is None else r,
        }

    barrier = pltpu.get_barrier_semaphore()

    def hello(dev):
        pl.semaphore_signal(barrier, inc=1, device_id=dev, device_id_type=MESH)

    for d in range(1, S):
        hello(at(section=lax.rem(me + d, S)))
    hello(at(r=other_row))

    @pl.when(has_left)
    def _():
        hello(at(c=col - 1))
        hello(at(c=col - 1, r=other_row))

    @pl.when(has_right)
    def _():
        hello(at(c=col + 1))
        hello(at(c=col + 1, r=other_row))

    K = w_ref.shape[0]
    half = K // 2
    piece = half // PIECES

    own_w = pltpu.make_async_copy(w_ref, wall.at[me], loc_sem.at[0])
    own_w.start()
    own_f = pltpu.make_async_copy(
        f_ref.at[micro],
        fwin.at[pl.ds(row * halo, R), pl.ds(hb, CL)],
        loc_sem.at[1],
    )
    own_f.start()

    for b in range(2):
        for mem in range(2):
            zeros = jnp.zeros((DILATION_RATE * NC, TAPS * C), jnp.bfloat16)
            act[b, mem, 0 : DILATION_RATE * NC, :] = zeros
            act[b, mem, (DILATION_RATE + NR) * NC :, :] = zeros

    greeted = 1 + (S - 1) + 2 * has_left.astype(jnp.int32) + 2 * has_right.astype(jnp.int32)
    pl.semaphore_wait(barrier, greeted)

    def remote(src, dst, s_sem, r_sem, dev):
        return pltpu.make_async_remote_copy(
            src_ref=src, dst_ref=dst, send_sem=s_sem, recv_sem=r_sem,
            device_id=dev, device_id_type=MESH,
        )

    rows_here = pl.ds(row * halo, R)
    rows_out = pl.ds((1 - row) * (R - halo), halo)
    rows_in = pl.ds(row * R, halo)
    mid = pl.ds(hb, CL)
    lcols, rcols = pl.ds(0, hb), pl.ds(hb + CL, hb)
    first, last = pl.ds(0, hb), pl.ds(CL - hb, hb)
    mine = f_ref.at[micro]
    to_left = remote(mine.at[:, first], fwin.at[rows_here, rcols], hs_sem.at[0], hr_sem.at[0], at(c=col - 1))
    to_right = remote(mine.at[:, last], fwin.at[rows_here, lcols], hs_sem.at[1], hr_sem.at[1], at(c=col + 1))
    to_row = remote(mine.at[rows_out], fwin.at[rows_in, mid], hs_sem.at[2], hr_sem.at[2], at(r=other_row))
    to_dl = remote(mine.at[rows_out, first], fwin.at[rows_in, rcols], hs_sem.at[3], hr_sem.at[3], at(c=col - 1, r=other_row))
    to_dr = remote(mine.at[rows_out, last], fwin.at[rows_in, lcols], hs_sem.at[4], hr_sem.at[4], at(c=col + 1, r=other_row))
    to_row.start()

    @pl.when(has_left)
    def _():
        to_left.start()
        to_dl.start()

    @pl.when(has_right)
    def _():
        to_right.start()
        to_dr.start()

    to_sib = remote(w_ref, wall.at[me], bs_sem, br_sem, at(section=sib))
    to_sib.start()

    def twin(k):
        a, b, res, bit = my_pair, k, 0, 1
        while bit < pairs:
            res = res + bit * lax.rem(a // bit + b // bit, 2)
            bit *= 2
        return 2 * res + low

    def part(h, j):
        return pl.ds(pl.multiple_of(h * half + j * piece, 16), piece)

    def xcopy(k, j):
        return remote(w_ref.at[part(row, j)], wall.at[me, part(row, j)],
                      xs_sem.at[k, j], xr_sem.at[k, j], at(section=twin(k)))

    def send_own():
        for k in range(1, pairs):
            for j in range(PIECES):
                xcopy(k, j).start()

    pl.when(low == 0)(send_own)

    def ycopy(t, k, j, h):
        slot = wall.at[t, part(h, j)]
        return remote(slot, slot, ys_sem.at[k, j], yr_sem.at[k, j], at(r=other_row))

    def ccopy(t, k, j, first):
        slot = wall.at[t, part(row if first else other_row, j)]
        n = 0 if first else 1
        return remote(slot, slot, cs_sem.at[k, n, j], cr_sem.at[k, n, j], at(section=sib))

    def pass_on(l, pieces):
        for k in range(1, pairs):
            @pl.when(twin(k) == l)
            def _(k=k):
                for j in pieces:
                    slot = wall.at[l, part(row, j)]
                    remote(slot, slot, xs_sem.at[k, j], xr_sem.at[k, j], at(section=l)).wait_recv()
                    ycopy(l, k, j, row).start()
                    ccopy(l, k, j, True).start()

    def complete(l):
        @pl.when(me == l)
        def _():
            own_w.wait()

        @pl.when(sib == l)
        def _():
            to_sib.wait_recv()

        for k in range(1, pairs):
            @pl.when(twin(k) == l)
            def _(k=k):
                for j in range(PIECES):
                    ycopy(l, k, j, other_row).wait_recv()
                    ccopy(l, k, j, False).start()

            @pl.when(twin(k) + 1 - 2 * low == l)
            def _(k=k):
                for j in range(PIECES):
                    ccopy(l, k, j, True).wait_recv()
                if l == 0:
                    pl.when(low == 1)(send_own)
                for j in range(PIECES):
                    ccopy(l, k, j, False).wait_recv()

    own_f.wait()
    to_row.wait()

    @pl.when(has_left)
    def _():
        to_left.wait_send()
        to_dl.wait_send()
        to_right.wait_recv()
        to_dr.wait_recv()

    @pl.when(has_right)
    def _():
        to_right.wait_send()
        to_dr.wait_send()
        to_left.wait_recv()
        to_dl.wait_recv()

    def in_map_only(v):
        return jnp.concatenate(
            [
                jnp.where(has_left, v[:, :halo], 0.0),
                v[:, halo : halo + CL],
                jnp.where(has_right, v[:, halo + CL :], 0.0),
            ],
            axis=1,
        )

    def put(b, mem, at_row, y, rows):
        m = rows * NC
        sl = pl.ds(pl.multiple_of((at_row + DILATION_RATE) * NC, 16), m)
        center = y.astype(jnp.bfloat16)
        left = pltpu.roll(center, DILATION_RATE, 0)
        right = pltpu.roll(center, m - DILATION_RATE, 0)
        for mm in mem:
            act[b, mm, sl, 0:C] = left if mm == 0 else right
            act[b, mm, sl, C : 2 * C] = center
            act[b, mm, sl, 2 * C : 3 * C] = right if mm == 0 else left

    off = hb - halo
    for i in range(0, NR, 4):
        v = fwin[i : i + 4].astype(jnp.float32)[:, off : off + NC, :]
        v = in_map_only(v)
        put(0, (0, 1), i, v.reshape(4 * NC, C), 4)

    early, late = range(PIECES // 2), range(PIECES // 2, PIECES)
    pass_on(0, range(PIECES))
    for l in range(S):
        complete(l)
        if l < S - 1:
            pass_on(l + 1, early)
        n = NR - DILATION_RATE * (l + 1)
        r0 = row * (NR - n)
        chunk = n // 2
        m = chunk * NC
        cur, nxt = l % 2, (l + 1) % 2
        for q in range(2):
            base = r0 + q * chunk
            if q == 1 and l < S - 1:
                pass_on(l + 1, late)
            ys = []
            for mem in range(2):
                lhs = jnp.concatenate(
                    [act[cur, mem, pl.ds(pl.multiple_of((base + DILATION_RATE * ky) * NC, 16), m), :] for ky in range(TAPS)],
                    axis=1,
                )
                acc = jnp.dot(lhs, wall[l], preferred_element_type=jnp.float32)
                res = act[cur, mem, pl.ds(pl.multiple_of((base + DILATION_RATE) * NC, 16), m), C : 2 * C]
                y = residual_scale * (res.astype(jnp.float32) + jnp.maximum(acc, 0.0))
                y = in_map_only(y.reshape(chunk, NC, C))
                y = y.astype(jnp.bfloat16).astype(jnp.float32)
                if l < S - 1:
                    put(nxt, (mem,), base, y.reshape(m, C), chunk)
                ys.append(y[:, halo : halo + CL, :])
            stage[l, q * chunk : (q + 1) * chunk] = ys[0].astype(jnp.bfloat16)
            d = ys[0] - ys[1]
            d = (d * d).reshape(chunk * CL, C)
            sums = lax.dot_general(
                jnp.ones((8, C), jnp.float32), d, (((1,), (1,)), ((), ())),
                preferred_element_type=jnp.float32,
            )
            lstage[l, :, q * chunk * CL : (q + 1) * chunk * CL] = sums

        if l == 0:
            pl.when(me == 1)(send_own)

        src = stage.at[l, pl.ds(row * (n - R), R)]

        @pl.when(jnp.logical_and(replica == l % group, me != l))
        def _(l=l, src=src):
            remote(src, out_ref.at[micro], os_sem.at[l], or_sem.at[micro], at(section=l)).start()
            remote(lstage.at[l], loss_ref.at[micro], ls_sem.at[l], lr_sem.at[micro], at(section=l)).start()

        @pl.when(jnp.logical_and(replica == l % group, me == l))
        def _(l=l, src=src):
            pltpu.make_async_copy(src, out_ref.at[micro], loc_sem.at[2]).start()
            pltpu.make_async_copy(lstage.at[l], loss_ref.at[micro], loc_sem.at[3]).start()

    for k in range(1, pairs):
        for j in range(PIECES):
            xcopy(k, j).wait_send()
            ycopy(twin(k), k, j, row).wait_send()
            ccopy(twin(k), k, j, True).wait_send()
            ccopy(twin(k), k, j, False).wait_send()
    to_sib.wait_send()

    for l in range(S):
        n = NR - DILATION_RATE * (l + 1)
        src = stage.at[l, pl.ds(row * (n - R), R)]

        @pl.when(jnp.logical_and(replica == l % group, me != l))
        def _(l=l, src=src):
            remote(src, out_ref.at[micro], os_sem.at[l], or_sem.at[micro], at(section=l)).wait_send()
            remote(lstage.at[l], loss_ref.at[micro], ls_sem.at[l], lr_sem.at[micro], at(section=l)).wait_send()

        @pl.when(jnp.logical_and(replica == l % group, me == l))
        def _(l=l, src=src):
            pltpu.make_async_copy(src, out_ref.at[micro], loc_sem.at[2]).wait()
            pltpu.make_async_copy(lstage.at[l], loss_ref.at[micro], loc_sem.at[3]).wait()

    for b in range(M):
        sender = b + M * lax.rem(me, group)

        @pl.when(sender != me)
        def _(b=b, sender=sender):
            remote(out_ref.at[b], out_ref.at[b], os_sem.at[0], or_sem.at[b], at(section=sender)).wait_recv()
            remote(loss_ref.at[b], loss_ref.at[b], ls_sem.at[0], lr_sem.at[b], at(section=sender)).wait_recv()


def local(features, conv_weight, tissue):
    S = lax.axis_size("section")
    n_col = lax.axis_size("col")
    M, R, CL, C = features.shape
    halo = DILATION_RATE * S
    hb = -(-halo // 16) * 16
    NR, NC = R + halo, CL + 2 * halo
    taps = conv_weight.shape[1]
    K = taps * taps * C
    pairs = S // 2
    lanes = -(-NR * CL // 128) * 128
    cfg = (S, M, R, CL, C, n_col, halo, hb, NR, NC)
    anyspec = pl.BlockSpec(memory_space=pl.ANY)
    dma = pltpu.SemaphoreType.DMA
    out, sums = pl.pallas_call(
        functools.partial(kernel, cfg),
        out_shape=(
            jax.ShapeDtypeStruct((M, R, CL, C), jnp.bfloat16),
            jax.ShapeDtypeStruct((M, 8, lanes), jnp.float32),
        ),
        in_specs=[anyspec, anyspec],
        out_specs=(anyspec, anyspec),
        scratch_shapes=[
            pltpu.VMEM((NR, CL + 2 * hb, C), jnp.bfloat16),
            pltpu.VMEM((S, K, C), jnp.bfloat16),
            pltpu.VMEM((2, 2, (NR + 2 * DILATION_RATE) * NC, taps * C), jnp.bfloat16),
            pltpu.VMEM((S, NR, CL, C), jnp.bfloat16),
            pltpu.VMEM((S, 8, lanes), jnp.float32),
            dma((5,)), dma((5,)),
            dma((pairs, PIECES)), dma((pairs, PIECES)),
            dma((pairs, PIECES)), dma((pairs, PIECES)),
            dma, dma,
            dma((pairs, 2, PIECES)), dma((pairs, 2, PIECES)),
            dma((S,)), dma((M,)),
            dma((S,)), dma((M,)),
            dma((4,)),
        ],
        compiler_params=pltpu.CompilerParams(
            collective_id=0, has_side_effects=True, vmem_limit_bytes=60 * 1024 * 1024
        ),
    )(features, conv_weight.reshape(K, C))
    layer = lax.axis_index("section")
    start = lax.axis_index("row") * (halo - DILATION_RATE * (layer + 1))
    own = lax.dynamic_slice_in_dim(sums[:, 0], start * CL, R * CL, axis=1).reshape(M, R, CL)
    loss = tissue.astype(jnp.float32) * (own * (1.0 / C))
    return out[None], loss[None]


def solution(mesh):
    return jax.shard_map(
        local,
        mesh=mesh,
        in_specs=(
            P(None, "row", "col", None),
            P("section", None, None, None, None),
            P(None, "row", "col"),
        ),
        out_specs=(P("section", None, "row", "col", None), P("section", None, "row", "col")),
        check_vma=False,
    )
```
